32 devices in a mesh: group: 4 (over y, core), depth: 8 (over z, x).
Axes of the slice: x: 2, y: 2, z: 4, core: 2. Of those that a mesh axis runs over, the one named last changes fastest.
Arguments:
- emission: bfloat16 [8, 128, 32, 1024], P('depth', 'group'), may hold values from 0.099609375 to 10
- opacity: bfloat16 [8, 128, 32, 1024], P('depth', 'group'), may hold values from 0.01 to 40
- brick_list: int32 [8, 1024, 8], P('depth', 'group'), may hold values from 0 to 127
- list_count: int32 [8, 1024], P('depth', 'group'), may hold values from 1 to 8
Outputs:
- radiance_image: float32 [1024, 128], P(('group', 'depth'))
- transmittance: float32 [1024, 128], P(('group', 'depth'))
The draws below stay inside these ranges and needn't reach their ends.
Inputs may be any that keep to these rules, and one draw needn't show every extreme that they name: `brick_list`: entries of a list at and beyond its count are ignored.
All inputs are finite; a program needn't handle non-finite values.
Results may differ from the reference program's by a relative error of at most 0.0003.
Values may be sent and summed in bfloat16 or wider, within the bound.
A program may use at most 128 MiB of HBM per device.

```python
import math
import jax
import jax.numpy as jnp
from jax import lax

CELLS = 32
RAYS = 128
LIST = 8
PIXELS = 1024
SLABS = 8
ROW_BRICKS = 128
TILES = 1024


def draw_opacity(key, part):
    brick_key = jax.random.fold_in(key, 17)
    cell_key = jax.random.fold_in(key, 29)
    full_shape = (SLABS, ROW_BRICKS, CELLS, PIXELS)
    lowest_scale = 0.05
    cell_values = jnp.exp(jax.random.uniform(cell_key, full_shape, jnp.float32, math.log(0.2), math.log(2.0)))
    brick_scale = jnp.exp(jax.random.uniform(brick_key, (SLABS, ROW_BRICKS, 1, 1), jnp.float32, math.log(lowest_scale), math.log(20.0)))
    return (brick_scale * cell_values).astype(jnp.bfloat16)


def touch_ends(values, key, least, high):
    longest = values.shape.index(max(values.shape))
    spots = []
    for shift in (0, 1):
        where = [jax.random.randint(jax.random.fold_in(key, axis), (), 0, length) for axis, length in enumerate(values.shape)]
        where[longest] = (where[longest] + shift) % values.shape[longest]
        spots.append(tuple(where))
    return values.at[spots[0]].set(least).at[spots[1]].set(high)


def shard_levels(own_key, shape, split, smallest, largest):
    loudness, own = 1.0, jax.random.fold_in(own_key, 6)
    for axis_at, blocks in split:
        heights = jnp.exp(jax.random.uniform(jax.random.fold_in(own, axis_at), (blocks,), jnp.float32, smallest / len(split), largest / len(split)))
        loudness = loudness * jnp.repeat(heights, shape[axis_at] // blocks).reshape([-1 if axis == axis_at else 1 for axis in range(len(shape))])
    return loudness


def setup_inputs(seed: int = 0) -> dict:
    keys = jax.random.split(jax.random.key(seed), 5)
    return {
        "emission": jnp.clip(jnp.exp(math.log(10.0) - 4.609084 * jax.random.uniform(keys[0], (SLABS, ROW_BRICKS, CELLS, PIXELS), jnp.float32) ** shard_levels(keys[0], (SLABS, ROW_BRICKS, CELLS, PIXELS), ((0, 8), (1, 4)), -0.2, 0.2)), 0.099609375, 10.0).astype(jnp.bfloat16),
        "opacity": draw_opacity(jax.random.fold_in(keys[4], 71), 0),
        "brick_list": touch_ends(jax.random.randint(keys[2], (SLABS, TILES, LIST), 0, ROW_BRICKS), jax.random.fold_in(keys[2], 1), 0, ROW_BRICKS - 1).astype(jnp.int32),
        "list_count": touch_ends(jax.random.randint(keys[3], (SLABS, TILES), 1, LIST + 1), jax.random.fold_in(keys[3], 1), 1, LIST).astype(jnp.int32),
    }


EXTINCTION = 2.0


def integrate(emission, opacity, extinct_scale):
    step_depth = opacity.astype(jnp.float32) * extinct_scale
    front_depth = jnp.cumsum(step_depth, axis=-2) - step_depth
    radiance = jnp.sum(emission.astype(jnp.float32) * (1.0 - jnp.exp(-step_depth)) * jnp.exp(-front_depth), axis=-2)
    return radiance, jnp.sum(step_depth, axis=-2)


def reference(emission, opacity, brick_list, list_count):
    extinct_scale = EXTINCTION / (CELLS * LIST * SLABS)
    sub_tiles = (CELLS * CELLS) // RAYS
    tile_ids = jnp.arange(TILES, dtype=jnp.int32)
    slot_ids = jnp.arange(LIST, dtype=jnp.int32)

    def one_slab(inputs):
        emit_slab, opac_slab, list_slab, count_slab = inputs
        radiance, optical = integrate(emit_slab, opac_slab, extinct_scale)
        table_light = radiance.reshape(ROW_BRICKS * sub_tiles, RAYS)
        table_depth = optical.reshape(ROW_BRICKS * sub_tiles, RAYS)
        rows_index = list_slab * sub_tiles + (tile_ids % sub_tiles)[:, None]
        live_mask = (slot_ids[None, :] < count_slab[:, None])[..., None]
        entry_light = jnp.where(live_mask, table_light[rows_index], jnp.float32(0.0))
        entry_depth = jnp.where(live_mask, table_depth[rows_index], jnp.float32(0.0))
        ahead_depth = jnp.cumsum(entry_depth, axis=1) - entry_depth
        return jnp.sum(entry_light * jnp.exp(-ahead_depth), axis=1), jnp.sum(entry_depth, axis=1)

    slab_light, slab_depth = lax.map(one_slab, (emission, opacity, brick_list, list_count))
    ahead_depth = jnp.cumsum(slab_depth, axis=0) - slab_depth
    radiance_image = jnp.sum(jnp.exp(-ahead_depth) * slab_light, axis=0)
    return radiance_image, jnp.exp(-jnp.sum(slab_depth, axis=0))
```

```python
import functools
import math

import jax
import jax.numpy as jnp
from jax import lax
from jax.experimental import pallas as pl
from jax.experimental.pallas import tpu as pltpu
from jax.sharding import PartitionSpec as P

RAYS = 128
EXTINCTION = 2.0
MESH = pl.DeviceIdType.MESH
ROWS = 8


def peer_order(n):
    if n % 2:
        return [(0, k) for k in range(1, n)] + [(0, 0)], 1, n
    chips = n // 2
    far = sorted(range(chips), key=lambda k: -min(k, chips - k))
    return [(dy, dc) for dy in far for dc in ((1, 0) if dy == 0 else (0, 1))], chips, 2


def kernel(
    n_group,
    n_depth,
    cells,
    slots,
    bricks,
    pixels,
    tiles,
    emission,
    opacity,
    brick_list,
    counts,
    image_out,
    trans_out,
    emit_buf,
    opac_buf,
    piece,
    table,
    list_rows,
    list_cols,
    slab_buf,
    recv_buf,
    final,
    emit_sem,
    opac_sem,
    piece_send,
    piece_recv,
    list_send,
    list_recv,
    slab_send,
    slab_recv,
):
    my_group = lax.axis_index("group")
    my_depth = lax.axis_index("depth")
    sub = pixels // RAYS
    share = pixels // n_group
    classes = share // RAYS
    own = tiles // n_depth
    steps = own // sub
    rows = classes * steps
    total_bricks = bricks * n_group
    scale = EXTINCTION / (cells * slots * n_depth)

    offsets, chips, cores = peer_order(n_group)
    my_chip, my_core = my_group // cores, my_group % cores
    order = [lax.rem(my_chip + dy, chips) * cores + lax.rem(my_core + dc, cores) for dy, dc in offsets]

    loads = []
    for at, peer in enumerate(order):
        lanes = pl.ds(pl.multiple_of(peer * share, RAYS), share)
        loads.append(
            (
                pltpu.make_async_copy(emission.at[0, :, :, lanes], emit_buf.at[at], emit_sem.at[at]),
                pltpu.make_async_copy(opacity.at[0, :, :, lanes], opac_buf.at[at], opac_sem.at[at]),
            )
        )
    for pair in loads:
        pair[1].start()
        pair[0].start()

    barrier = pltpu.get_barrier_semaphore()

    @pl.loop(1, n_group * n_depth)
    def _(shift):
        to = lax.rem(my_group * n_depth + my_depth + shift, n_group * n_depth)
        pl.semaphore_signal(
            barrier, inc=1, device_id=(to // n_depth, lax.rem(to, n_depth)), device_id_type=MESH
        )

    slot_ids = lax.broadcasted_iota(jnp.int32, (slots, tiles), 0)
    flipped = jnp.transpose(brick_list[0].astype(jnp.float32))
    list_rows[my_group] = jnp.where(slot_ids < counts[...], flipped, -1.0)

    height = ROWS * cells
    row = lax.broadcasted_iota(jnp.int32, (height, height), 0)
    column = lax.broadcasted_iota(jnp.int32, (height, height), 1)
    cell = row // ROWS
    gap = column - (row - cell * ROWS) * cells
    move = jnp.where(gap == cell, 1.0, 0.0).astype(jnp.bfloat16)
    running = jnp.where((gap >= 0) & (gap <= cell), 1.0, 0.0).astype(jnp.bfloat16)

    pl.semaphore_wait(barrier, n_group * n_depth - 1)

    list_copies = []
    for at in range(n_group - 1):
        list_copies.append(
            pltpu.make_async_remote_copy(
                src_ref=list_rows.at[my_group],
                dst_ref=list_rows.at[my_group],
                send_sem=list_send.at[at],
                recv_sem=list_recv.at[my_group],
                device_id=(order[at], my_depth),
                device_id_type=MESH,
            )
        )
        list_copies[-1].start()

    def integrate(at, first):
        opac = opac_buf[at, pl.ds(first, ROWS)].reshape(height, share)
        emit = emit_buf[at, pl.ds(first, ROWS)].reshape(height, share)
        depth = jnp.dot(running, opac, preferred_element_type=jnp.float32)
        source = jnp.dot(move, emit, preferred_element_type=jnp.float32)
        before = jnp.ones((ROWS, share), jnp.float32)
        light = jnp.zeros((ROWS, share), jnp.float32)
        for k in range(cells):
            after = jnp.exp2(depth[k * ROWS : (k + 1) * ROWS] * (-scale * math.log2(math.e)))
            light = light + source[k * ROWS : (k + 1) * ROWS] * (before - after)
            before = after
        return light, depth[(cells - 1) * ROWS :] * scale

    piece_copies = []
    for at, peer in enumerate(order):
        loads[at][1].wait()
        loads[at][0].wait()

        @pl.loop(0, bricks // (2 * ROWS))
        def _(block):
            first = pl.multiple_of(block * 2 * ROWS, 2 * ROWS)
            parts = [integrate(at, first), integrate(at, first + ROWS)]
            for value in range(2):
                whole = jnp.concatenate([parts[0][value], parts[1][value]], axis=0)
                high = whole.astype(jnp.bfloat16)
                low = (whole - high.astype(jnp.float32)).astype(jnp.bfloat16)
                for c in range(classes):
                    lanes = slice(c * RAYS, (c + 1) * RAYS)
                    at_lanes = pl.ds(value * RAYS, RAYS)
                    piece[at, c, 0, pl.ds(first, 2 * ROWS), at_lanes] = high[:, lanes]
                    piece[at, c, 1, pl.ds(first, 2 * ROWS), at_lanes] = low[:, lanes]

        mine = pl.ds(pl.multiple_of(my_group * bricks, 2 * ROWS), bricks)
        if at < n_group - 1:
            copy = pltpu.make_async_remote_copy(
                src_ref=piece.at[at],
                dst_ref=table.at[:, :, mine, :],
                send_sem=piece_send.at[at],
                recv_sem=piece_recv.at[my_group],
                device_id=(peer, my_depth),
                device_id_type=MESH,
            )
            copy.start()
            piece_copies.append(copy)
        else:
            table[:, :, mine, :] = piece[at]

    for at in range(n_group - 1):
        list_copies[at].wait_send()
        pltpu.make_async_remote_copy(
            src_ref=list_rows.at[order[at]],
            dst_ref=list_rows.at[order[at]],
            send_sem=list_send.at[at],
            recv_sem=list_recv.at[order[at]],
            device_id=(order[at], my_depth),
            device_id_type=MESH,
        ).wait_recv()
    for s in range(n_group):
        list_cols[s] = jnp.transpose(jnp.concatenate([list_rows[s]] * (RAYS // slots), axis=0))

    for at in range(n_group - 1):
        piece_copies[at].wait_send()
        theirs = pl.ds(pl.multiple_of(order[at] * bricks, 2 * ROWS), bricks)
        pltpu.make_async_remote_copy(
            src_ref=piece.at[at],
            dst_ref=table.at[:, :, theirs, :],
            send_sem=piece_send.at[at],
            recv_sem=piece_recv.at[order[at]],
            device_id=(order[at], my_depth),
            device_id_type=MESH,
        ).wait_recv()

    count = steps * n_depth
    brick_ids = lax.broadcasted_iota(jnp.int32, (count, total_bricks), 1).astype(jnp.float32)

    def slab_copy(s, d):
        return pltpu.make_async_remote_copy(
            src_ref=slab_buf.at[s, d],
            dst_ref=recv_buf.at[my_depth, my_group],
            send_sem=slab_send.at[s, d],
            recv_sem=slab_recv.at[my_depth, my_group],
            device_id=(s, d),
            device_id_type=MESH,
        )

    for s in order:
        for c in range(classes):
            mark = my_group * classes + c
            entries = jnp.concatenate(
                [list_cols[s, pl.ds(mark + sub * i, n_depth, stride=own), :] for i in range(steps)], axis=0
            )
            picks = [
                jnp.where(entries[:, l : l + 1] == brick_ids, 1.0, 0.0).astype(jnp.bfloat16) for l in range(slots)
            ]
            picks = jnp.concatenate(picks, axis=0)
            picks = jnp.concatenate([picks, picks], axis=1)
            found = jnp.dot(
                picks, table[c].reshape(2 * total_bricks, 2 * RAYS), preferred_element_type=jnp.float32
            )
            light = jnp.zeros((count, RAYS), jnp.float32)
            depth = jnp.zeros((count, RAYS), jnp.float32)
            for l in range(slots - 1, -1, -1):
                entry_light = found[l * count : (l + 1) * count, :RAYS]
                entry_depth = found[l * count : (l + 1) * count, RAYS:]
                light = entry_light + jnp.exp(-entry_depth) * light
                depth = depth + entry_depth
            for value, data in enumerate((light, depth)):
                for i in range(steps):
                    slab_buf[s, :, value * rows + c * steps + i, :] = data[i * n_depth : (i + 1) * n_depth]

        @pl.loop(0, n_depth)
        def _(d):
            @pl.when(jnp.logical_or(s != my_group, d != my_depth))
            def _():
                slab_copy(s, d).start()

    recv_buf[my_depth, my_group] = slab_buf[my_group, my_depth]

    @pl.loop(0, n_group * n_depth)
    def _(which):
        g, d = which // n_depth, lax.rem(which, n_depth)

        @pl.when(jnp.logical_or(g != my_group, d != my_depth))
        def _():
            slab_copy(g, d).wait_send()
            pltpu.make_async_remote_copy(
                src_ref=slab_buf.at[g, d],
                dst_ref=recv_buf.at[d, g],
                send_sem=slab_send.at[g, d],
                recv_sem=slab_recv.at[d, g],
                device_id=(g, d),
                device_id_type=MESH,
            ).wait_recv()

    light = jnp.zeros((n_group, rows, RAYS), jnp.float32)
    depth = jnp.zeros((n_group, rows, RAYS), jnp.float32)
    for d in range(n_depth - 1, -1, -1):
        slab_light = recv_buf[d, :, :rows, :]
        slab_depth = recv_buf[d, :, rows:, :]
        light = slab_light + jnp.exp(-slab_depth) * light
        depth = depth + slab_depth
    for g in range(n_group):
        final[0, g * rows : (g + 1) * rows, :] = light[g]
        final[1, g * rows : (g + 1) * rows, :] = jnp.exp(-depth[g])
    for i in range(steps):
        image_out[i * sub : (i + 1) * sub, :] = final[0, pl.ds(i, sub, stride=steps), :]
        trans_out[i * sub : (i + 1) * sub, :] = final[1, pl.ds(i, sub, stride=steps), :]


def local(emission, opacity, brick_list, list_count):
    n_group, n_depth = lax.axis_size("group"), lax.axis_size("depth")
    _, bricks, cells, pixels = emission.shape
    _, tiles, slots = brick_list.shape
    share = pixels // n_group
    classes = share // RAYS
    own = tiles // n_depth
    rows = classes * own // (pixels // RAYS)
    any_space = pl.BlockSpec(memory_space=pl.ANY)
    in_vmem = pl.BlockSpec(memory_space=pltpu.VMEM)
    dma = pltpu.SemaphoreType.DMA
    image, trans = pl.pallas_call(
        functools.partial(kernel, n_group, n_depth, cells, slots, bricks, pixels, tiles),
        out_shape=[jax.ShapeDtypeStruct((own, RAYS), jnp.float32)] * 2,
        in_specs=[any_space, any_space, in_vmem, in_vmem],
        out_specs=[in_vmem, in_vmem],
        scratch_shapes=[
            pltpu.VMEM((n_group, bricks, cells, share), jnp.bfloat16),
            pltpu.VMEM((n_group, bricks, cells, share), jnp.bfloat16),
            pltpu.VMEM((n_group, classes, 2, bricks, 2 * RAYS), jnp.bfloat16),
            pltpu.VMEM((classes, 2, bricks * n_group, 2 * RAYS), jnp.bfloat16),
            pltpu.VMEM((n_group, slots, tiles), jnp.float32),
            pltpu.VMEM((n_group, tiles, RAYS), jnp.float32),
            pltpu.VMEM((n_group, n_depth, 2 * rows, RAYS), jnp.float32),
            pltpu.VMEM((n_depth, n_group, 2 * rows, RAYS), jnp.float32),
            pltpu.VMEM((2, n_group * rows, RAYS), jnp.float32),
            dma((n_group,)),
            dma((n_group,)),
            dma((n_group,)),
            dma((n_group,)),
            dma((n_group,)),
            dma((n_group,)),
            dma((n_group, n_depth)),
            dma((n_depth, n_group)),
        ],
        compiler_params=pltpu.CompilerParams(
            collective_id=0, has_side_effects=True, vmem_limit_bytes=48 * 1024 * 1024
        ),
    )(emission, opacity, brick_list, list_count)
    return image, trans


def solution(mesh):
    return jax.shard_map(
        local,
        mesh=mesh,
        in_specs=(
            P("depth", "group", None, None),
            P("depth", "group", None, None),
            P("depth", "group", None),
            P("depth", "group"),
        ),
        out_specs=(P(("group", "depth"), None), P(("group", "depth"), None)),
        check_vma=False,
    )
```

```python
import functools
import math

import jax
import jax.numpy as jnp
from jax import lax
from jax.experimental import pallas as pl
from jax.experimental.pallas import tpu as pltpu
from jax.sharding import PartitionSpec as P

RAYS = 128
EXTINCTION = 2.0
MESH = pl.DeviceIdType.MESH
ROWS = 8


def peer_order(n):
    if n % 2:
        return [(0, k) for k in range(1, n)] + [(0, 0)], 1, n
    chips = n // 2
    far = sorted(range(chips), key=lambda k: -min(k, chips - k))
    return [(dy, dc) for dy in far for dc in ((1, 0) if dy == 0 else (0, 1))], chips, 2


def kernel(
    n_group,
    n_depth,
    cells,
    slots,
    bricks,
    pixels,
    tiles,
    emission,
    opacity,
    brick_list,
    counts,
    image_out,
    trans_out,
    emit_buf,
    opac_buf,
    piece,
    table,
    list_rows,
    list_cols,
    slab_buf,
    recv_buf,
    final,
    list_in,
    count_row,
    small_sem,
    emit_sem,
    opac_sem,
    piece_send,
    piece_recv,
    list_send,
    list_recv,
    slab_send,
    slab_recv,
):
    my_group = lax.axis_index("group")
    my_depth = lax.axis_index("depth")
    sub = pixels // RAYS
    share = pixels // n_group
    classes = share // RAYS
    own = tiles // n_depth
    steps = own // sub
    rows = classes * steps
    total_bricks = bricks * n_group
    scale = EXTINCTION / (cells * slots * n_depth)

    offsets, chips, cores = peer_order(n_group)
    my_chip, my_core = my_group // cores, my_group % cores
    order = [lax.rem(my_chip + dy, chips) * cores + lax.rem(my_core + dc, cores) for dy, dc in offsets]

    small = (
        pltpu.make_async_copy(brick_list.at[0], list_in, small_sem.at[0]),
        pltpu.make_async_copy(counts, count_row, small_sem.at[1]),
    )
    for load in small:
        load.start()
    loads = []
    for at, peer in enumerate(order):
        lanes = pl.ds(pl.multiple_of(peer * share, RAYS), share)
        loads.append(
            (
                pltpu.make_async_copy(emission.at[0, :, :, lanes], emit_buf.at[at], emit_sem.at[at]),
                pltpu.make_async_copy(opacity.at[0, :, :, lanes], opac_buf.at[at], opac_sem.at[at]),
            )
        )
    for pair in loads:
        pair[1].start()
        pair[0].start()

    barrier = pltpu.get_barrier_semaphore()

    @pl.loop(1, n_group * n_depth)
    def _(shift):
        to = lax.rem(my_group * n_depth + my_depth + shift, n_group * n_depth)
        pl.semaphore_signal(
            barrier, inc=1, device_id=(to // n_depth, lax.rem(to, n_depth)), device_id_type=MESH
        )

    slot_ids = lax.broadcasted_iota(jnp.int32, (slots, tiles), 0)
    for load in small:
        load.wait()
    list_rows[my_group] = jnp.where(slot_ids < count_row[...], list_in[...].astype(jnp.float32), -1.0)

    height = ROWS * cells
    row = lax.broadcasted_iota(jnp.int32, (height, height), 0)
    column = lax.broadcasted_iota(jnp.int32, (height, height), 1)
    cell = row // ROWS
    gap = column - (row - cell * ROWS) * cells
    move = jnp.where(gap == cell, 1.0, 0.0).astype(jnp.bfloat16)
    running = jnp.where((gap >= 0) & (gap <= cell), 1.0, 0.0).astype(jnp.bfloat16)

    pl.semaphore_wait(barrier, n_group * n_depth - 1)

    list_copies = []
    for at in range(n_group - 1):
        list_copies.append(
            pltpu.make_async_remote_copy(
                src_ref=list_rows.at[my_group],
                dst_ref=list_rows.at[my_group],
                send_sem=list_send.at[at],
                recv_sem=list_recv.at[my_group],
                device_id=(order[at], my_depth),
                device_id_type=MESH,
            )
        )
        list_copies[-1].start()

    def integrate(at, first):
        opac = opac_buf[at, pl.ds(first, ROWS)].reshape(height, share)
        emit = emit_buf[at, pl.ds(first, ROWS)].reshape(height, share)
        depth = jnp.dot(running, opac, preferred_element_type=jnp.float32)
        source = jnp.dot(move, emit, preferred_element_type=jnp.float32)
        before = jnp.ones((ROWS, share), jnp.float32)
        light = jnp.zeros((ROWS, share), jnp.float32)
        for k in range(cells):
            after = jnp.exp2(depth[k * ROWS : (k + 1) * ROWS] * (-scale * math.log2(math.e)))
            light = light + source[k * ROWS : (k + 1) * ROWS] * (before - after)
            before = after
        return light, depth[(cells - 1) * ROWS :] * scale

    piece_copies = []
    for at, peer in enumerate(order):
        loads[at][1].wait()
        loads[at][0].wait()

        @pl.loop(0, bricks // (2 * ROWS))
        def _(block):
            first = pl.multiple_of(block * 2 * ROWS, 2 * ROWS)
            parts = [integrate(at, first), integrate(at, first + ROWS)]
            for value in range(2):
                whole = jnp.concatenate([parts[0][value], parts[1][value]], axis=0)
                high = whole.astype(jnp.bfloat16)
                low = (whole - high.astype(jnp.float32)).astype(jnp.bfloat16)
                for c in range(classes):
                    lanes = slice(c * RAYS, (c + 1) * RAYS)
                    at_lanes = pl.ds(value * RAYS, RAYS)
                    piece[at, c, 0, pl.ds(first, 2 * ROWS), at_lanes] = high[:, lanes]
                    piece[at, c, 1, pl.ds(first, 2 * ROWS), at_lanes] = low[:, lanes]

        mine = pl.ds(pl.multiple_of(my_group * bricks, 2 * ROWS), bricks)
        if at < n_group - 1:
            copy = pltpu.make_async_remote_copy(
                src_ref=piece.at[at],
                dst_ref=table.at[:, :, mine, :],
                send_sem=piece_send.at[at],
                recv_sem=piece_recv.at[my_group],
                device_id=(peer, my_depth),
                device_id_type=MESH,
            )
            copy.start()
            piece_copies.append(copy)
        else:
            table[:, :, mine, :] = piece[at]

    for at in range(n_group - 1):
        list_copies[at].wait_send()
        pltpu.make_async_remote_copy(
            src_ref=list_rows.at[order[at]],
            dst_ref=list_rows.at[order[at]],
            send_sem=list_send.at[at],
            recv_sem=list_recv.at[order[at]],
            device_id=(order[at], my_depth),
            device_id_type=MESH,
        ).wait_recv()
    for s in range(n_group):
        list_cols[s] = jnp.transpose(jnp.concatenate([list_rows[s]] * (RAYS // slots), axis=0))

    for at in range(n_group - 1):
        piece_copies[at].wait_send()
        theirs = pl.ds(pl.multiple_of(order[at] * bricks, 2 * ROWS), bricks)
        pltpu.make_async_remote_copy(
            src_ref=piece.at[at],
            dst_ref=table.at[:, :, theirs, :],
            send_sem=piece_send.at[at],
            recv_sem=piece_recv.at[order[at]],
            device_id=(order[at], my_depth),
            device_id_type=MESH,
        ).wait_recv()

    count = steps * n_depth
    brick_ids = lax.broadcasted_iota(jnp.int32, (count, total_bricks), 1).astype(jnp.float32)

    def slab_copy(s, d):
        return pltpu.make_async_remote_copy(
            src_ref=slab_buf.at[s, d],
            dst_ref=recv_buf.at[my_depth, my_group],
            send_sem=slab_send.at[s, d],
            recv_sem=slab_recv.at[my_depth, my_group],
            device_id=(s, d),
            device_id_type=MESH,
        )

    for s in order:
        for c in range(classes):
            mark = my_group * classes + c
            entries = jnp.concatenate(
                [list_cols[s, pl.ds(mark + sub * i, n_depth, stride=own), :] for i in range(steps)], axis=0
            )
            picks = [
                jnp.where(entries[:, l : l + 1] == brick_ids, 1.0, 0.0).astype(jnp.bfloat16) for l in range(slots)
            ]
            picks = jnp.concatenate(picks, axis=0)
            picks = jnp.concatenate([picks, picks], axis=1)
            found = jnp.dot(
                picks, table[c].reshape(2 * total_bricks, 2 * RAYS), preferred_element_type=jnp.float32
            )
            light = jnp.zeros((count, RAYS), jnp.float32)
            depth = jnp.zeros((count, RAYS), jnp.float32)
            for l in range(slots - 1, -1, -1):
                entry_light = found[l * count : (l + 1) * count, :RAYS]
                entry_depth = found[l * count : (l + 1) * count, RAYS:]
                light = entry_light + jnp.exp(-entry_depth) * light
                depth = depth + entry_depth
            for value, data in enumerate((light, depth)):
                for i in range(steps):
                    slab_buf[s, :, value * rows + c * steps + i, :] = data[i * n_depth : (i + 1) * n_depth]

        @pl.loop(0, n_depth)
        def _(d):
            @pl.when(jnp.logical_or(s != my_group, d != my_depth))
            def _():
                slab_copy(s, d).start()

    recv_buf[my_depth, my_group] = slab_buf[my_group, my_depth]

    @pl.loop(0, n_group * n_depth)
    def _(which):
        g, d = which // n_depth, lax.rem(which, n_depth)

        @pl.when(jnp.logical_or(g != my_group, d != my_depth))
        def _():
            slab_copy(g, d).wait_send()
            pltpu.make_async_remote_copy(
                src_ref=slab_buf.at[g, d],
                dst_ref=recv_buf.at[d, g],
                send_sem=slab_send.at[g, d],
                recv_sem=slab_recv.at[d, g],
                device_id=(g, d),
                device_id_type=MESH,
            ).wait_recv()

    light = jnp.zeros((n_group, rows, RAYS), jnp.float32)
    depth = jnp.zeros((n_group, rows, RAYS), jnp.float32)
    for d in range(n_depth - 1, -1, -1):
        slab_light = recv_buf[d, :, :rows, :]
        slab_depth = recv_buf[d, :, rows:, :]
        light = slab_light + jnp.exp(-slab_depth) * light
        depth = depth + slab_depth
    for g in range(n_group):
        final[0, g * rows : (g + 1) * rows, :] = light[g]
        final[1, g * rows : (g + 1) * rows, :] = jnp.exp(-depth[g])
    for i in range(steps):
        image_out[i * sub : (i + 1) * sub, :] = final[0, pl.ds(i, sub, stride=steps), :]
        trans_out[i * sub : (i + 1) * sub, :] = final[1, pl.ds(i, sub, stride=steps), :]


def local(emission, opacity, brick_list, list_count):
    n_group, n_depth = lax.axis_size("group"), lax.axis_size("depth")
    _, bricks, cells, pixels = emission.shape
    _, tiles, slots = brick_list.shape
    share = pixels // n_group
    classes = share // RAYS
    own = tiles // n_depth
    rows = classes * own // (pixels // RAYS)
    in_hbm = pl.BlockSpec(memory_space=pltpu.HBM)
    in_vmem = pl.BlockSpec(memory_space=pltpu.VMEM)
    dma = pltpu.SemaphoreType.DMA
    image, trans = pl.pallas_call(
        functools.partial(kernel, n_group, n_depth, cells, slots, bricks, pixels, tiles),
        out_shape=[jax.ShapeDtypeStruct((own, RAYS), jnp.float32)] * 2,
        in_specs=[in_hbm] * 4,
        out_specs=[in_vmem, in_vmem],
        scratch_shapes=[
            pltpu.VMEM((n_group, bricks, cells, share), jnp.bfloat16),
            pltpu.VMEM((n_group, bricks, cells, share), jnp.bfloat16),
            pltpu.VMEM((n_group, classes, 2, bricks, 2 * RAYS), jnp.bfloat16),
            pltpu.VMEM((classes, 2, bricks * n_group, 2 * RAYS), jnp.bfloat16),
            pltpu.VMEM((n_group, slots, tiles), jnp.float32),
            pltpu.VMEM((n_group, tiles, RAYS), jnp.float32),
            pltpu.VMEM((n_group, n_depth, 2 * rows, RAYS), jnp.float32),
            pltpu.VMEM((n_depth, n_group, 2 * rows, RAYS), jnp.float32),
            pltpu.VMEM((2, n_group * rows, RAYS), jnp.float32),
            pltpu.VMEM((slots, tiles), jnp.int32),
            pltpu.VMEM((1, tiles), jnp.int32),
            dma((2,)),
            dma((n_group,)),
            dma((n_group,)),
            dma((n_group,)),
            dma((n_group,)),
            dma((n_group,)),
            dma((n_group,)),
            dma((n_group, n_depth)),
            dma((n_depth, n_group)),
        ],
        compiler_params=pltpu.CompilerParams(
            collective_id=0, has_side_effects=True, vmem_limit_bytes=60 * 1024 * 1024
        ),
    )(emission, opacity, jnp.swapaxes(brick_list, 1, 2), list_count)
    return image, trans


def solution(mesh):
    return jax.shard_map(
        local,
        mesh=mesh,
        in_specs=(
            P("depth", "group", None, None),
            P("depth", "group", None, None),
            P("depth", "group", None),
            P("depth", "group"),
        ),
        out_specs=(P(("group", "depth"), None), P(("group", "depth"), None)),
        check_vma=False,
    )
```

```python
import functools
import math

import jax
import jax.numpy as jnp
from jax import lax
from jax.experimental import pallas as pl
from jax.experimental.pallas import tpu as pltpu
from jax.sharding import PartitionSpec as P

RAYS = 128
EXTINCTION = 2.0
MESH = pl.DeviceIdType.MESH
BEFORE = 1
ROWS = 8


def peer_order(n):
    if n % 2:
        return [(0, k) for k in range(1, n)] + [(0, 0)], 1, n
    chips = n // 2
    far = sorted(range(chips), key=lambda k: -min(k, chips - k))
    return [(dy, dc) for dy in far for dc in ((1, 0) if dy == 0 else (0, 1))], chips, 2


def kernel(
    n_group,
    n_depth,
    cells,
    slots,
    bricks,
    pixels,
    tiles,
    emission,
    opacity,
    brick_list,
    counts,
    image_out,
    emit_buf,
    opac_buf,
    piece,
    table,
    list_rows,
    list_cols,
    slab_buf,
    recv_buf,
    final,
    list_in,
    count_row,
    small_sem,
    emit_sem,
    opac_sem,
    piece_send,
    piece_recv,
    list_send,
    list_recv,
    slab_send,
    slab_recv,
):
    my_group = lax.axis_index("group")
    my_depth = lax.axis_index("depth")
    sub = pixels // RAYS
    share = pixels // n_group
    classes = share // RAYS
    own = tiles // n_depth
    steps = own // sub
    rows = classes * steps
    total_bricks = bricks * n_group
    scale = EXTINCTION / (cells * slots * n_depth)

    offsets, chips, cores = peer_order(n_group)
    my_chip, my_core = my_group // cores, my_group % cores
    order = [lax.rem(my_chip + dy, chips) * cores + lax.rem(my_core + dc, cores) for dy, dc in offsets]

    small = (
        pltpu.make_async_copy(brick_list.at[0], list_in, small_sem.at[0]),
        pltpu.make_async_copy(counts, count_row, small_sem.at[1]),
    )
    for load in small:
        load.start()
    loads = []
    for at, peer in enumerate(order):
        lanes = pl.ds(pl.multiple_of(peer * share, RAYS), share)
        loads.append(
            (
                pltpu.make_async_copy(emission.at[0, :, :, lanes], emit_buf.at[at], emit_sem.at[at]),
                pltpu.make_async_copy(opacity.at[0, :, :, lanes], opac_buf.at[at], opac_sem.at[at]),
            )
        )
    for pair in loads:
        pair[1].start()
        pair[0].start()

    barrier = pltpu.get_barrier_semaphore()

    @pl.loop(1, n_group * n_depth)
    def _(shift):
        to = lax.rem(my_group * n_depth + my_depth + shift, n_group * n_depth)
        pl.semaphore_signal(
            barrier, inc=1, device_id=(to // n_depth, lax.rem(to, n_depth)), device_id_type=MESH
        )

    slot_ids = lax.broadcasted_iota(jnp.int32, (slots, tiles), 0)
    for load in small:
        load.wait()
    list_rows[my_group] = jnp.where(slot_ids < count_row[...], list_in[...].astype(jnp.float32), -1.0)

    height = ROWS * cells
    row = lax.broadcasted_iota(jnp.int32, (height, height), 0)
    column = lax.broadcasted_iota(jnp.int32, (height, height), 1)
    cell = row // ROWS
    gap = column - (row - cell * ROWS) * cells
    move = jnp.where(gap == cell, 1.0, 0.0).astype(jnp.bfloat16)
    running = jnp.where((gap >= 0) & (gap <= cell), 1.0, 0.0).astype(jnp.bfloat16)

    list_copies = []

    def enter():
        pl.semaphore_wait(barrier, n_group * n_depth - 1)
        for at in range(n_group - 1):
            list_copies.append(
                pltpu.make_async_remote_copy(
                    src_ref=list_rows.at[my_group],
                    dst_ref=list_rows.at[my_group],
                    send_sem=list_send.at[at],
                    recv_sem=list_recv.at[my_group],
                    device_id=(order[at], my_depth),
                    device_id_type=MESH,
                )
            )
            list_copies[-1].start()

    def integrate(at, first):
        opac = opac_buf[at, pl.ds(first, ROWS)].reshape(height, share)
        emit = emit_buf[at, pl.ds(first, ROWS)].reshape(height, share)
        depth = jnp.dot(running, opac, preferred_element_type=jnp.float32)
        source = jnp.dot(move, emit, preferred_element_type=jnp.float32)
        before = jnp.ones((ROWS, share), jnp.float32)
        light = jnp.zeros((ROWS, share), jnp.float32)
        for k in range(cells):
            after = jnp.exp2(depth[k * ROWS : (k + 1) * ROWS] * (-scale * math.log2(math.e)))
            light = light + source[k * ROWS : (k + 1) * ROWS] * (before - after)
            before = after
        return light, depth[(cells - 1) * ROWS :] * scale

    piece_copies = []
    mine = pl.ds(pl.multiple_of(my_group * bricks, 2 * ROWS), bricks)

    def send_piece(at):
        return pltpu.make_async_remote_copy(
            src_ref=piece.at[at],
            dst_ref=table.at[:, :, mine, :],
            send_sem=piece_send.at[at],
            recv_sem=piece_recv.at[my_group],
            device_id=(order[at], my_depth),
            device_id_type=MESH,
        )

    for at, peer in enumerate(order):
        loads[at][1].wait()
        loads[at][0].wait()

        @pl.loop(0, bricks // (2 * ROWS))
        def _(block):
            first = pl.multiple_of(block * 2 * ROWS, 2 * ROWS)
            parts = [integrate(at, first), integrate(at, first + ROWS)]
            for value in range(2):
                whole = jnp.concatenate([parts[0][value], parts[1][value]], axis=0)
                high = whole.astype(jnp.bfloat16)
                low = (whole - high.astype(jnp.float32)).astype(jnp.bfloat16)
                for c in range(classes):
                    lanes = slice(c * RAYS, (c + 1) * RAYS)
                    at_lanes = pl.ds(value * RAYS, RAYS)
                    piece[at, c, 0, pl.ds(first, 2 * ROWS), at_lanes] = high[:, lanes]
                    piece[at, c, 1, pl.ds(first, 2 * ROWS), at_lanes] = low[:, lanes]

        if at + 1 == BEFORE:
            enter()
        if at + 1 >= BEFORE:
            for done in range(at + 1 if at + 1 == BEFORE else 1):
                done = done if at + 1 == BEFORE else at
                if done < n_group - 1:
                    piece_copies.append(send_piece(done))
                    piece_copies[-1].start()
    table[:, :, mine, :] = piece[n_group - 1]

    for at in range(n_group - 1):
        list_copies[at].wait_send()
        pltpu.make_async_remote_copy(
            src_ref=list_rows.at[order[at]],
            dst_ref=list_rows.at[order[at]],
            send_sem=list_send.at[at],
            recv_sem=list_recv.at[order[at]],
            device_id=(order[at], my_depth),
            device_id_type=MESH,
        ).wait_recv()
    for s in range(n_group):
        list_cols[s] = jnp.transpose(jnp.concatenate([list_rows[s]] * (RAYS // slots), axis=0))

    for at in range(n_group - 1):
        piece_copies[at].wait_send()
        theirs = pl.ds(pl.multiple_of(order[at] * bricks, 2 * ROWS), bricks)
        pltpu.make_async_remote_copy(
            src_ref=piece.at[at],
            dst_ref=table.at[:, :, theirs, :],
            send_sem=piece_send.at[at],
            recv_sem=piece_recv.at[order[at]],
            device_id=(order[at], my_depth),
            device_id_type=MESH,
        ).wait_recv()

    count = steps * n_depth
    brick_ids = lax.broadcasted_iota(jnp.int32, (count, total_bricks), 1).astype(jnp.float32)

    def slab_copy(s, d):
        return pltpu.make_async_remote_copy(
            src_ref=slab_buf.at[s, d],
            dst_ref=recv_buf.at[my_depth, my_group],
            send_sem=slab_send.at[s, d],
            recv_sem=slab_recv.at[my_depth, my_group],
            device_id=(s, d),
            device_id_type=MESH,
        )

    for s in order:
        for c in range(classes):
            mark = my_group * classes + c
            entries = jnp.concatenate(
                [list_cols[s, pl.ds(mark + sub * i, n_depth, stride=own), :] for i in range(steps)], axis=0
            )
            picks = [
                jnp.where(entries[:, l : l + 1] == brick_ids, 1.0, 0.0).astype(jnp.bfloat16) for l in range(slots)
            ]
            picks = jnp.concatenate(picks, axis=0)
            picks = jnp.concatenate([picks, picks], axis=1)
            found = jnp.dot(
                picks, table[c].reshape(2 * total_bricks, 2 * RAYS), preferred_element_type=jnp.float32
            )
            light = jnp.zeros((count, RAYS), jnp.float32)
            depth = jnp.zeros((count, RAYS), jnp.float32)
            for l in range(slots - 1, -1, -1):
                entry_light = found[l * count : (l + 1) * count, :RAYS]
                entry_depth = found[l * count : (l + 1) * count, RAYS:]
                light = entry_light + jnp.exp(-entry_depth) * light
                depth = depth + entry_depth
            for value, data in enumerate((light, depth)):
                for i in range(steps):
                    slab_buf[s, :, value * rows + c * steps + i, :] = data[i * n_depth : (i + 1) * n_depth]

        @pl.loop(0, n_depth)
        def _(d):
            @pl.when(jnp.logical_or(s != my_group, d != my_depth))
            def _():
                slab_copy(s, d).start()

    recv_buf[my_depth, my_group] = slab_buf[my_group, my_depth]

    @pl.loop(0, n_group * n_depth)
    def _(which):
        g, d = which // n_depth, lax.rem(which, n_depth)

        @pl.when(jnp.logical_or(g != my_group, d != my_depth))
        def _():
            slab_copy(g, d).wait_send()
            pltpu.make_async_remote_copy(
                src_ref=slab_buf.at[g, d],
                dst_ref=recv_buf.at[d, g],
                send_sem=slab_send.at[g, d],
                recv_sem=slab_recv.at[d, g],
                device_id=(g, d),
                device_id_type=MESH,
            ).wait_recv()

    light = jnp.zeros((n_group, rows, RAYS), jnp.float32)
    depth = jnp.zeros((n_group, rows, RAYS), jnp.float32)
    for d in range(n_depth - 1, -1, -1):
        slab_light = recv_buf[d, :, :rows, :]
        slab_depth = recv_buf[d, :, rows:, :]
        light = slab_light + jnp.exp(-slab_depth) * light
        depth = depth + slab_depth
    for g in range(n_group):
        final[0, g * rows : (g + 1) * rows, :] = light[g]
        final[1, g * rows : (g + 1) * rows, :] = depth[g]
    for i in range(steps):
        image_out[0, i * sub : (i + 1) * sub, :] = final[0, pl.ds(i, sub, stride=steps), :]
        image_out[1, i * sub : (i + 1) * sub, :] = final[1, pl.ds(i, sub, stride=steps), :]


def local(emission, opacity, brick_list, list_count):
    n_group, n_depth = lax.axis_size("group"), lax.axis_size("depth")
    _, bricks, cells, pixels = emission.shape
    _, tiles, slots = brick_list.shape
    share = pixels // n_group
    classes = share // RAYS
    own = tiles // n_depth
    rows = classes * own // (pixels // RAYS)
    in_hbm = pl.BlockSpec(memory_space=pltpu.HBM)
    in_vmem = pl.BlockSpec(memory_space=pltpu.VMEM)
    dma = pltpu.SemaphoreType.DMA
    both = pl.pallas_call(
        functools.partial(kernel, n_group, n_depth, cells, slots, bricks, pixels, tiles),
        out_shape=jax.ShapeDtypeStruct((2, own, RAYS), jnp.float32),
        in_specs=[in_hbm] * 4,
        out_specs=in_vmem,
        scratch_shapes=[
            pltpu.VMEM((n_group, bricks, cells, share), jnp.bfloat16),
            pltpu.VMEM((n_group, bricks, cells, share), jnp.bfloat16),
            pltpu.VMEM((n_group, classes, 2, bricks, 2 * RAYS), jnp.bfloat16),
            pltpu.VMEM((classes, 2, bricks * n_group, 2 * RAYS), jnp.bfloat16),
            pltpu.VMEM((n_group, slots, tiles), jnp.float32),
            pltpu.VMEM((n_group, tiles, RAYS), jnp.float32),
            pltpu.VMEM((n_group, n_depth, 2 * rows, RAYS), jnp.float32),
            pltpu.VMEM((n_depth, n_group, 2 * rows, RAYS), jnp.float32),
            pltpu.VMEM((2, n_group * rows, RAYS), jnp.float32),
            pltpu.VMEM((slots, tiles), jnp.int32),
            pltpu.VMEM((1, tiles), jnp.int32),
            dma((2,)),
            dma((n_group,)),
            dma((n_group,)),
            dma((n_group,)),
            dma((n_group,)),
            dma((n_group,)),
            dma((n_group,)),
            dma((n_group, n_depth)),
            dma((n_depth, n_group)),
        ],
        compiler_params=pltpu.CompilerParams(
            collective_id=0, has_side_effects=True, vmem_limit_bytes=40000 * 1024
        ),
    )(pltpu.with_memory_space_constraint(emission, pltpu.HBM), pltpu.with_memory_space_constraint(opacity, pltpu.HBM), pltpu.with_memory_space_constraint(jnp.swapaxes(brick_list, 1, 2), pltpu.HBM), pltpu.with_memory_space_constraint(list_count, pltpu.HBM))
    return both[0], jnp.exp(-both[1])


def solution(mesh):
    return jax.shard_map(
        local,
        mesh=mesh,
        in_specs=(
            P("depth", "group", None, None),
            P("depth", "group", None, None),
            P("depth", "group", None),
            P("depth", "group"),
        ),
        out_specs=(P(("group", "depth"), None), P(("group", "depth"), None)),
        check_vma=False,
    )
```

```python
import functools
import math

import jax
import jax.numpy as jnp
from jax import lax
from jax.experimental import pallas as pl
from jax.experimental.pallas import tpu as pltpu
from jax.sharding import PartitionSpec as P

RAYS = 128
EXTINCTION = 2.0
MESH = pl.DeviceIdType.MESH
BEFORE = 1
ROWS = 8


def peer_order(n):
    if n % 2:
        return [(0, k) for k in range(1, n)] + [(0, 0)], 1, n
    chips = n // 2
    far = sorted(range(chips), key=lambda k: -min(k, chips - k))
    return [(dy, dc) for dy in far for dc in ((1, 0) if dy == 0 else (0, 1))], chips, 2


def kernel(
    n_group,
    n_depth,
    cells,
    slots,
    bricks,
    pixels,
    tiles,
    emission,
    opacity,
    brick_list,
    counts,
    image_out,
    emit_buf,
    opac_buf,
    piece,
    table,
    list_rows,
    list_cols,
    slab_buf,
    recv_buf,
    final,
    list_in,
    count_row,
    small_sem,
    emit_sem,
    opac_sem,
    piece_send,
    piece_recv,
    list_send,
    list_recv,
    slab_send,
    slab_recv,
):
    my_group = lax.axis_index("group")
    my_depth = lax.axis_index("depth")
    sub = pixels // RAYS
    share = pixels // n_group
    classes = share // RAYS
    own = tiles // n_depth
    steps = own // sub
    rows = classes * steps
    total_bricks = bricks * n_group
    scale = EXTINCTION / (cells * slots * n_depth)

    offsets, chips, cores = peer_order(n_group)
    my_chip, my_core = my_group // cores, my_group % cores
    order = [lax.rem(my_chip + dy, chips) * cores + lax.rem(my_core + dc, cores) for dy, dc in offsets]

    small = (
        pltpu.make_async_copy(brick_list.at[0], list_in, small_sem.at[0]),
        pltpu.make_async_copy(counts, count_row, small_sem.at[1]),
    )
    for load in small:
        load.start()
    loads = []
    for at, peer in enumerate(order):
        lanes = pl.ds(pl.multiple_of(peer * share, RAYS), share)
        loads.append(
            (
                pltpu.make_async_copy(emission.at[0, :, :, lanes], emit_buf.at[at], emit_sem.at[at]),
                pltpu.make_async_copy(opacity.at[0, :, :, lanes], opac_buf.at[at], opac_sem.at[at]),
            )
        )
    for pair in loads:
        pair[1].start()
        pair[0].start()

    barrier = pltpu.get_barrier_semaphore()

    @pl.loop(1, n_group * n_depth)
    def _(shift):
        to = lax.rem(my_group * n_depth + my_depth + shift, n_group * n_depth)
        pl.semaphore_signal(
            barrier, inc=1, device_id=(to // n_depth, lax.rem(to, n_depth)), device_id_type=MESH
        )

    slot_ids = lax.broadcasted_iota(jnp.int32, (slots, tiles), 0)
    for load in small:
        load.wait()
    list_rows[my_group] = jnp.where(slot_ids < count_row[...], list_in[...].astype(jnp.float32), -1.0)

    height = ROWS * cells
    row = lax.broadcasted_iota(jnp.int32, (height, height), 0)
    column = lax.broadcasted_iota(jnp.int32, (height, height), 1)
    cell = row // ROWS
    gap = column - (row - cell * ROWS) * cells
    move = jnp.where(gap == cell, 1.0, 0.0).astype(jnp.bfloat16)
    running = jnp.where((gap >= 0) & (gap <= cell), 1.0, 0.0).astype(jnp.bfloat16)

    list_copies = []

    def enter():
        pl.semaphore_wait(barrier, n_group * n_depth - 1)
        for at in range(n_group - 1):
            list_copies.append(
                pltpu.make_async_remote_copy(
                    src_ref=list_rows.at[my_group],
                    dst_ref=list_rows.at[my_group],
                    send_sem=list_send.at[at],
                    recv_sem=list_recv.at[my_group],
                    device_id=(order[at], my_depth),
                    device_id_type=MESH,
                )
            )
            list_copies[-1].start()

    def integrate(at, first):
        opac = opac_buf[at, pl.ds(first, ROWS)].reshape(height, share)
        emit = emit_buf[at, pl.ds(first, ROWS)].reshape(height, share)
        depth = jnp.dot(running, opac, preferred_element_type=jnp.float32)
        source = jnp.dot(move, emit, preferred_element_type=jnp.float32)
        before = jnp.ones((ROWS, share), jnp.float32)
        light = jnp.zeros((ROWS, share), jnp.float32)
        for k in range(cells):
            after = jnp.exp2(depth[k * ROWS : (k + 1) * ROWS] * (-scale * math.log2(math.e)))
            light = light + source[k * ROWS : (k + 1) * ROWS] * (before - after)
            before = after
        return light, depth[(cells - 1) * ROWS :] * scale

    piece_copies = []
    mine = pl.ds(pl.multiple_of(my_group * bricks, 2 * ROWS), bricks)

    def send_piece(at):
        return pltpu.make_async_remote_copy(
            src_ref=piece.at[at],
            dst_ref=table.at[:, :, mine, :],
            send_sem=piece_send.at[at],
            recv_sem=piece_recv.at[my_group],
            device_id=(order[at], my_depth),
            device_id_type=MESH,
        )

    for at, peer in enumerate(order):
        loads[at][1].wait()
        loads[at][0].wait()

        @pl.loop(0, bricks // (2 * ROWS))
        def _(block):
            first = pl.multiple_of(block * 2 * ROWS, 2 * ROWS)
            parts = [integrate(at, first), integrate(at, first + ROWS)]
            for value in range(2):
                whole = jnp.concatenate([parts[0][value], parts[1][value]], axis=0)
                high = whole.astype(jnp.bfloat16)
                low = (whole - high.astype(jnp.float32)).astype(jnp.bfloat16)
                for c in range(classes):
                    lanes = slice(c * RAYS, (c + 1) * RAYS)
                    at_lanes = pl.ds(value * RAYS, RAYS)
                    piece[at, c, 0, pl.ds(first, 2 * ROWS), at_lanes] = high[:, lanes]
                    piece[at, c, 1, pl.ds(first, 2 * ROWS), at_lanes] = low[:, lanes]

        if at + 1 == BEFORE:
            enter()
        if at + 1 >= BEFORE:
            for done in range(at + 1 if at + 1 == BEFORE else 1):
                done = done if at + 1 == BEFORE else at
                if done < n_group - 1:
                    piece_copies.append(send_piece(done))
                    piece_copies[-1].start()
    table[:, :, mine, :] = piece[n_group - 1]

    for at in range(n_group - 1):
        list_copies[at].wait_send()
        pltpu.make_async_remote_copy(
            src_ref=list_rows.at[order[at]],
            dst_ref=list_rows.at[order[at]],
            send_sem=list_send.at[at],
            recv_sem=list_recv.at[order[at]],
            device_id=(order[at], my_depth),
            device_id_type=MESH,
        ).wait_recv()
    for s in range(n_group):
        list_cols[s] = jnp.transpose(jnp.concatenate([list_rows[s]] * (RAYS // slots), axis=0))

    for at in range(n_group - 1):
        piece_copies[at].wait_send()
        theirs = pl.ds(pl.multiple_of(order[at] * bricks, 2 * ROWS), bricks)
        pltpu.make_async_remote_copy(
            src_ref=piece.at[at],
            dst_ref=table.at[:, :, theirs, :],
            send_sem=piece_send.at[at],
            recv_sem=piece_recv.at[order[at]],
            device_id=(order[at], my_depth),
            device_id_type=MESH,
        ).wait_recv()

    count = steps * n_depth
    brick_ids = lax.broadcasted_iota(jnp.int32, (count, total_bricks), 1).astype(jnp.float32)

    def slab_copy(s, d):
        return pltpu.make_async_remote_copy(
            src_ref=slab_buf.at[s, d],
            dst_ref=recv_buf.at[my_depth, my_group],
            send_sem=slab_send.at[s, d],
            recv_sem=slab_recv,
            device_id=(s, d),
            device_id_type=MESH,
        )

    for s in order:
        for c in range(classes):
            mark = my_group * classes + c
            entries = jnp.concatenate(
                [list_cols[s, pl.ds(mark + sub * i, n_depth, stride=own), :] for i in range(steps)], axis=0
            )
            picks = [
                jnp.where(entries[:, l : l + 1] == brick_ids, 1.0, 0.0).astype(jnp.bfloat16) for l in range(slots)
            ]
            picks = jnp.concatenate(picks, axis=0)
            picks = jnp.concatenate([picks, picks], axis=1)
            found = jnp.dot(
                picks, table[c].reshape(2 * total_bricks, 2 * RAYS), preferred_element_type=jnp.float32
            )
            light = jnp.zeros((count, RAYS), jnp.float32)
            depth = jnp.zeros((count, RAYS), jnp.float32)
            for l in range(slots - 1, -1, -1):
                entry_light = found[l * count : (l + 1) * count, :RAYS]
                entry_depth = found[l * count : (l + 1) * count, RAYS:]
                light = entry_light + jnp.exp(-entry_depth) * light
                depth = depth + entry_depth
            for value, data in enumerate((light, depth)):
                for i in range(steps):
                    slab_buf[s, :, value * rows + c * steps + i, :] = data[i * n_depth : (i + 1) * n_depth]

        @pl.loop(0, n_depth)
        def _(d):
            @pl.when(jnp.logical_or(s != my_group, d != my_depth))
            def _():
                slab_copy(s, d).start()

    pltpu.make_async_copy(
        slab_buf.at[my_group, my_depth], recv_buf.at[my_depth, my_group], slab_recv
    ).start()

    @pl.loop(0, n_group * n_depth)
    def _(which):
        g, d = which // n_depth, lax.rem(which, n_depth)

        @pl.when(jnp.logical_or(g != my_group, d != my_depth))
        def _():
            slab_copy(g, d).wait_send()

    pltpu.make_async_copy(recv_buf, recv_buf, slab_recv).wait()

    light = jnp.zeros((n_group, rows, RAYS), jnp.float32)
    depth = jnp.zeros((n_group, rows, RAYS), jnp.float32)
    for d in range(n_depth - 1, -1, -1):
        slab_light = recv_buf[d, :, :rows, :]
        slab_depth = recv_buf[d, :, rows:, :]
        light = slab_light + jnp.exp(-slab_depth) * light
        depth = depth + slab_depth
    for g in range(n_group):
        final[0, g * rows : (g + 1) * rows, :] = light[g]
        final[1, g * rows : (g + 1) * rows, :] = depth[g]
    for i in range(steps):
        image_out[0, i * sub : (i + 1) * sub, :] = final[0, pl.ds(i, sub, stride=steps), :]
        image_out[1, i * sub : (i + 1) * sub, :] = final[1, pl.ds(i, sub, stride=steps), :]


def local(emission, opacity, brick_list, list_count):
    n_group, n_depth = lax.axis_size("group"), lax.axis_size("depth")
    _, bricks, cells, pixels = emission.shape
    _, tiles, slots = brick_list.shape
    share = pixels // n_group
    classes = share // RAYS
    own = tiles // n_depth
    rows = classes * own // (pixels // RAYS)
    in_hbm = pl.BlockSpec(memory_space=pltpu.HBM)
    in_vmem = pl.BlockSpec(memory_space=pltpu.VMEM)
    dma = pltpu.SemaphoreType.DMA
    both = pl.pallas_call(
        functools.partial(kernel, n_group, n_depth, cells, slots, bricks, pixels, tiles),
        out_shape=jax.ShapeDtypeStruct((2, own, RAYS), jnp.float32),
        in_specs=[in_hbm] * 4,
        out_specs=in_vmem,
        scratch_shapes=[
            pltpu.VMEM((n_group, bricks, cells, share), jnp.bfloat16),
            pltpu.VMEM((n_group, bricks, cells, share), jnp.bfloat16),
            pltpu.VMEM((n_group, classes, 2, bricks, 2 * RAYS), jnp.bfloat16),
            pltpu.VMEM((classes, 2, bricks * n_group, 2 * RAYS), jnp.bfloat16),
            pltpu.VMEM((n_group, slots, tiles), jnp.float32),
            pltpu.VMEM((n_group, tiles, RAYS), jnp.float32),
            pltpu.VMEM((n_group, n_depth, 2 * rows, RAYS), jnp.float32),
            pltpu.VMEM((n_depth, n_group, 2 * rows, RAYS), jnp.float32),
            pltpu.VMEM((2, n_group * rows, RAYS), jnp.float32),
            pltpu.VMEM((slots, tiles), jnp.int32),
            pltpu.VMEM((1, tiles), jnp.int32),
            dma((2,)),
            dma((n_group,)),
            dma((n_group,)),
            dma((n_group,)),
            dma((n_group,)),
            dma((n_group,)),
            dma((n_group,)),
            dma((n_group, n_depth)),
            dma(()),
        ],
        compiler_params=pltpu.CompilerParams(
            collective_id=0, has_side_effects=True, vmem_limit_bytes=40000 * 1024
        ),
    )(pltpu.with_memory_space_constraint(emission, pltpu.HBM), pltpu.with_memory_space_constraint(opacity, pltpu.HBM), pltpu.with_memory_space_constraint(jnp.swapaxes(brick_list, 1, 2), pltpu.HBM), pltpu.with_memory_space_constraint(list_count, pltpu.HBM))
    return both[0], jnp.exp(-both[1])


def solution(mesh):
    return jax.shard_map(
        local,
        mesh=mesh,
        in_specs=(
            P("depth", "group", None, None),
            P("depth", "group", None, None),
            P("depth", "group", None),
            P("depth", "group"),
        ),
        out_specs=(P(("group", "depth"), None), P(("group", "depth"), None)),
        check_vma=False,
    )
```
